128 devices in a mesh: seq: 32 (over z, y, core), dp: 4 (over x).
Axes of the slice: x: 4, y: 4, z: 4, core: 2. Of those that a mesh axis runs over, the one named last changes fastest.
Arguments:
- queries: bfloat16 [32768, 2048], P(('dp', 'seq')), parts along dimension 0, may hold values from -5 to 5
- keys: bfloat16 [32768, 128], P(('dp', 'seq')), parts along dimension 0, may hold values from -5 to 5
- values: bfloat16 [32768, 128], P(('dp', 'seq')), parts along dimension 0, may hold values from -5 to 5
- lengths: int32 [128], P('dp'), parts along dimension 0, may hold values from 1 to 2048, 8192 in all
- grad_out: bfloat16 [32768, 2048], P(('dp', 'seq')), parts along dimension 0, may hold values from -5 to 5
Outputs:
- attended: bfloat16 [32768, 2048], P(('dp', 'seq')), parts along dimension 0
- grad_queries: bfloat16 [32768, 2048], P(('dp', 'seq')), parts along dimension 0
- grad_keys: bfloat16 [32768, 128], P(('dp', 'seq')), parts along dimension 0
- grad_values: bfloat16 [32768, 128], P(('dp', 'seq')), parts along dimension 0
The draws below stay inside these ranges and needn't reach their ends.
There are 4 independent parts, one for each index of `dp`. The reference program is written for one: setup_inputs(seed, part) draws one part's arguments, and reference() takes and returns one part's arrays. A program takes and returns all parts, laid end to end along the dimension named above; each array names one. Nothing has to cross between parts.
Inputs may be any that keep to these rules, and one draw needn't show every extreme that they name: The lengths sum to 8192.
All inputs are finite; a program needn't handle non-finite values.
Results may differ from the reference program's by a relative error of at most 0.018.
Values may be sent and summed in bfloat16 or wider, within the bound.
A program may use at most 256 MiB of HBM per device.

```python
import math
import jax
import jax.numpy as jnp
import numpy as np
from jax import lax

H = 16
DH = 128
TOK_DEV = 256
SPAN = 8
MAXLEN = 2048
TOKENS = 8192
DOCS = 32
N_SEQ = 32


def draw_queries(key, part):
    noise = jnp.clip(jax.random.normal(jax.random.fold_in(key, 11), (TOKENS, H * DH), jnp.float32), -4.0, 4.0)
    return noise.astype(jnp.bfloat16)


def draw_keys(key, part):
    noise = jnp.clip(jax.random.normal(jax.random.fold_in(key, 21), (TOKENS, DH), jnp.float32), -4.0, 4.0)
    return noise.astype(jnp.bfloat16)


def steps_of(stream_key, dims, pieces, least, high):
    def one(dim, parts):
        draws = jax.random.uniform(jax.random.fold_in(jax.random.fold_in(stream_key, 6), dim), (parts,), jnp.float32, least / len(pieces), high / len(pieces))
        return jnp.repeat(jnp.exp(draws), dims[dim] // parts).reshape((-1,) + (1,) * (len(dims) - dim - 1))

    factor_of = one(*pieces[0])
    for cut in pieces[1:]:
        factor_of = factor_of * one(*cut)
    return factor_of


def length_profile(count, total, limit, skew):
    portions = [(1 << 20) // math.isqrt(grade ** skew) + 1 for grade in range(2, count + 1)]
    surplus, holding = total - limit - (count - 1), [1] * (count - 1)
    while surplus > 0:
        candidates = [i for i in range(count - 1) if holding[i] < limit]
        pool, budget = sum([portions[i] for i in candidates]), surplus
        for i in candidates:
            extra = min(limit - holding[i], max(1, budget * portions[i] // pool), surplus)
            holding[i] = holding[i] + extra
            surplus = surplus - extra
    return np.array([limit] + holding)


def uneven_parts(rng, number_of, total, limit, slope):
    if number_of == 2:
        one = jax.random.randint(rng, (), max(1, total - limit), min(limit, total - 1) + 1)
        return jnp.stack([one, total - one])
    sizes = jnp.asarray(length_profile(number_of, total, limit, slope), jnp.int32)
    twos = (number_of - 1) // 2
    source_of, sink = sizes[1:1 + 2 * twos:2], sizes[2:2 + 2 * twos:2]
    margin = jnp.minimum(source_of - 1, limit - sink)
    shifted = jax.random.randint(jax.random.fold_in(rng, 1), (twos,), 0, 1 << 20) % (margin + 1)
    sizes = sizes.at[1:1 + 2 * twos:2].set(source_of - shifted).at[2:2 + 2 * twos:2].set(sink + shifted)
    return sizes[jax.random.permutation(jax.random.fold_in(rng, 2), number_of)]


def gaussian(rng, shape, scale, bound, shards=(), kind=jnp.bfloat16):
    gain = steps_of(rng, shape, shards, -0.22, 0.18) if shards else 1.0
    entries = jax.random.normal(rng, shape, jnp.float32) * scale * gain
    return jnp.minimum(jnp.maximum(entries, -bound), bound).astype(kind)


def setup_inputs(seed: int = 0, part: int = 0) -> dict:
    seeds = jax.random.split(jax.random.key(seed), 6)
    part_splits = jax.random.split(jax.random.fold_in(seeds[5], part), 6)
    return {
        "queries": draw_queries(jax.random.fold_in(jax.random.fold_in(seeds[5], part), 71), part),
        "keys": draw_keys(jax.random.fold_in(jax.random.fold_in(seeds[5], part), 71), part),
        "values": gaussian(part_splits[2], (TOKENS, DH), 1.0, 5.0, ((0, 32),)),
        "lengths": uneven_parts(part_splits[3], DOCS, TOKENS, MAXLEN, 2).astype(jnp.int32),
        "grad_out": gaussian(part_splits[4], (TOKENS, H * DH), 1.0, 5.0, ((0, 32),)),
    }


NEG_FILL = -1.0e30


def reference(queries, keys, values, lengths, grad_out):
    score_scale = 1.0 / (DH ** 0.5)
    window_rows = (SPAN + 1) * TOK_DEV
    pad_rows = SPAN * TOK_DEV
    key_value = jnp.concatenate([keys, values], axis=1)
    padded = jnp.concatenate([jnp.zeros((pad_rows, 2 * DH), key_value.dtype), key_value], axis=0)
    doc_ends = jnp.cumsum(lengths).astype(jnp.int32)

    def one_block(grad_acc, block):
        first = (block * TOK_DEV).astype(jnp.int32)
        positions = first + jnp.arange(TOK_DEV, dtype=jnp.int32)
        doc_starts = jnp.max(jnp.where(doc_ends[None, :] <= positions[:, None], doc_ends[None, :], 0), axis=1)
        key_pos = first - pad_rows + jnp.arange(window_rows, dtype=jnp.int32)
        visible = (key_pos[None, :] >= doc_starts[:, None]) & (key_pos[None, :] <= positions[:, None])
        visible = jnp.broadcast_to(visible[:, None, :], (TOK_DEV, H, window_rows)).reshape(TOK_DEV * H, window_rows)
        section = lax.dynamic_slice_in_dim(padded, first, window_rows, 0)
        key_block = section[:, :DH]
        value_block = section[:, DH:]
        query_rows = lax.dynamic_slice_in_dim(queries, first, TOK_DEV, 0).reshape(TOK_DEV * H, DH)
        grad_rows = lax.dynamic_slice_in_dim(grad_out, first, TOK_DEV, 0).reshape(TOK_DEV * H, DH)
        scores = jnp.dot(query_rows, key_block.T, preferred_element_type=jnp.float32) * score_scale
        scores = jnp.where(visible, scores, NEG_FILL)
        top = jnp.max(scores, axis=1)
        total = jnp.sum(jnp.where(visible, jnp.exp(scores - top[:, None]), 0.0), axis=1)
        log_total = top + jnp.log(total)
        weights = jnp.where(visible, jnp.exp(scores - log_total[:, None]), 0.0)
        rounded = weights.astype(jnp.bfloat16)
        out_rows = jnp.dot(rounded, value_block, preferred_element_type=jnp.float32).astype(jnp.bfloat16)
        delta = jnp.sum(grad_rows.astype(jnp.float32) * out_rows.astype(jnp.float32), axis=1)
        grad_weights = jnp.dot(grad_rows, value_block.T, preferred_element_type=jnp.float32)
        grad_scores = (weights * (grad_weights - delta[:, None])).astype(jnp.bfloat16)
        grad_query = (score_scale * jnp.dot(grad_scores, key_block, preferred_element_type=jnp.float32)).astype(jnp.bfloat16)
        block_grad = jnp.concatenate([
            jnp.dot(grad_scores.T, query_rows, preferred_element_type=jnp.float32),
            jnp.dot(rounded.T, grad_rows, preferred_element_type=jnp.float32)], axis=1)
        current = lax.dynamic_slice_in_dim(grad_acc, first, window_rows, 0)
        grad_acc = lax.dynamic_update_slice_in_dim(grad_acc, current + block_grad, first, 0)
        return grad_acc, (out_rows.reshape(TOK_DEV, H * DH), grad_query.reshape(TOK_DEV, H * DH))

    start_acc = jnp.zeros((pad_rows + TOKENS, 2 * DH), jnp.float32)
    grad_acc, (outs, grads) = lax.scan(one_block, start_acc, jnp.arange(N_SEQ, dtype=jnp.int32))
    key_total = grad_acc[pad_rows:]
    attended = outs.reshape(TOKENS, H * DH)
    grad_queries = grads.reshape(TOKENS, H * DH)
    grad_keys = (score_scale * key_total[:, :DH]).astype(jnp.bfloat16)
    grad_values = key_total[:, DH:].astype(jnp.bfloat16)
    return (attended, grad_queries, grad_keys, grad_values)
```

```python
import functools
import math

import jax
import jax.numpy as jnp
from jax import lax
from jax.experimental import pallas as pl
from jax.experimental.pallas import tpu as pltpu
from jax.sharding import PartitionSpec as P

NEG_FILL = -1e30
ROWS_Y = 4
SLOTS = 9


def dot_nt(a, b):
    return lax.dot_general(a, b, (((1,), (1,)), ((), ())), preferred_element_type=jnp.float32)


def dot_nn(a, b):
    return lax.dot_general(a, b, (((1,), (0,)), ((), ())), preferred_element_type=jnp.float32)


def kernel(
    n_seq,
    heads,
    len_ref,
    q_hbm,
    k_hbm,
    v_hbm,
    g_hbm,
    o_hbm,
    dq_hbm,
    gk_ref,
    gv_ref,
    q_ref,
    g_ref,
    qt_ref,
    gt_ref,
    kv,
    s_ref,
    m_ref,
    del_ref,
    dq_acc,
    o_ref,
    ds_ref,
    bias,
    part,
    gs,
    gr,
    in_sem,
    out_sem,
    kv_send,
    kv_recv,
    g_send,
    g_recv,
):
    T, D = gk_ref.shape
    R = T * heads
    half = D
    scale = 1.0 / math.sqrt(D)
    scale2 = scale * math.log2(math.e)
    me = lax.axis_index("seq")
    core = lax.rem(me, 2)
    y = lax.rem(me // 2, ROWS_Y)
    row0 = me - (y * 2 + core)
    partner = row0 + y * 2 + (1 - core)
    z_next = lax.rem(me + 2 * ROWS_Y, n_seq)
    z_prev = lax.rem(me + n_seq - 2 * ROWS_Y, n_seq)

    def y_dev(d):
        return row0 + 2 * lax.rem(y + d, ROWS_Y) + core

    def head_copy(src, dst, h, sem):
        return pltpu.make_async_copy(src.at[:, pl.ds(h * D, D)], dst.at[pl.ds(h * T, T), :], sem)

    k_copy = pltpu.make_async_copy(k_hbm, kv.at[0, 0], in_sem.at[0])
    v_copy = pltpu.make_async_copy(v_hbm, kv.at[0, 1], in_sem.at[1])
    k_copy.start()
    v_copy.start()
    for h in range(heads):
        head_copy(q_hbm, q_ref, h, in_sem.at[2 + h]).start()
    for h in range(heads):
        head_copy(g_hbm, g_ref, h, in_sem.at[2 + heads + h]).start()

    barrier = pltpu.get_barrier_semaphore()
    for dev in (z_next, z_prev, partner, y_dev(1), y_dev(2), y_dev(3)):
        pl.semaphore_signal(
            barrier, inc=1, device_id={"seq": dev}, device_id_type=pl.DeviceIdType.MESH
        )

    def kv_to(src, dst, dev):
        return pltpu.make_async_remote_copy(
            src_ref=kv.at[src],
            dst_ref=kv.at[dst],
            send_sem=kv_send.at[dst],
            recv_sem=kv_recv.at[dst],
            device_id={"seq": dev},
            device_id_type=pl.DeviceIdType.MESH,
        )

    def grad_to(i, dev):
        return pltpu.make_async_remote_copy(
            src_ref=gs.at[i],
            dst_ref=gr.at[i],
            send_sem=g_send.at[i],
            recv_sem=g_recv.at[i],
            device_id={"seq": dev},
            device_id_type=pl.DeviceIdType.MESH,
        )

    k_copy.wait()
    v_copy.wait()
    pl.semaphore_wait(barrier, 6)
    kv_to(0, 1, z_next).start()
    for d in (1, 2, 3):

        @pl.when(y + d < ROWS_Y)
        def _():
            kv_to(0, 1 + d, y_dev(d)).start()

    @pl.when(core == 0)
    def _():
        kv_to(0, 5, partner).start()

    first = me * T
    pos = first + lax.broadcasted_iota(jnp.int32, (T, 128), 0)
    starts = jnp.zeros((T, 128), jnp.int32)
    end = jnp.int32(0)
    for i in range(len_ref.shape[0]):
        end = end + len_ref[i]
        starts = jnp.where(pos >= end, end, starts)
    ds_ref[...] = starts
    m_ref[...] = jnp.full(m_ref.shape, -3e38, jnp.float32)
    dq_acc[...] = jnp.zeros(dq_acc.shape, jnp.float32)
    for h in range(heads):
        head_copy(q_hbm, q_ref, h, in_sem.at[2 + h]).wait()
    for h in range(heads):
        head_copy(g_hbm, g_ref, h, in_sem.at[2 + heads + h]).wait()
    for c in range(4):
        w = R // 4
        qt_ref[:, c * w : (c + 1) * w] = q_ref[c * w : (c + 1) * w, :].T
        gt_ref[:, c * w : (c + 1) * w] = g_ref[c * w : (c + 1) * w, :].T

    def score_slot(slot, carry):
        @pl.when(slot >= 1)
        def _():
            kv_to(0, slot, me).wait_recv()

        @pl.when(slot == 1)
        def _():
            for d in (1, 2, 3):

                @pl.when(y + d >= ROWS_Y)
                def _():
                    kv_to(1, 1 + d, y_dev(d)).start()

            @pl.when(core == 1)
            def _():
                kv_to(1, 5, partner).start()

        @pl.when((slot >= 2) & (slot <= 4))
        def _():
            kv_to(slot, slot + 4, partner).start()

        same = jnp.where(slot == 1, 2 * ROWS_Y, 2 * (slot - 1))
        same = jnp.where(slot == 0, 0, same)
        other = jnp.where(core == 1, 2 * (slot - 5) + 1, 2 * (slot - 5) - 1)
        other = jnp.where((slot == 5) & (core == 0), 2 * ROWS_Y - 1, other)
        offset = jnp.where(slot >= 5, other, same)
        base = (me - offset) * T
        lo = ds_ref[...] - base
        hi = offset * T + lax.broadcasted_iota(jnp.int32, (T, 128), 0)
        col = lax.broadcasted_iota(jnp.int32, (T, 128), 1)
        for j in range(T // 128):
            cj = col + j * 128
            bias[:, j * 128 : (j + 1) * 128] = jnp.where(
                (cj >= lo) & (cj <= hi), 0.0, NEG_FILL
            )
        s = dot_nt(q_ref[...], kv[slot, 0]) * scale2
        for h in range(heads):
            rs = slice(h * T, (h + 1) * T)
            sh = s[rs] + bias[...]
            s_ref[slot, rs, :] = sh
            top = m_ref[rs, :]
            for j in range(T // 128):
                top = jnp.maximum(top, sh[:, j * 128 : (j + 1) * 128])
            m_ref[rs, :] = top
        return carry

    lax.fori_loop(0, SLOTS, score_slot, 0)

    per = 4

    def out_chunk(c, carry):
        for u in range(per):
            rs = pl.ds(pl.multiple_of((c * per + u) * T, T), T)
            m = jnp.max(m_ref[rs, :], axis=1, keepdims=True)
            total = jnp.zeros((T, 128), jnp.float32)
            acc = jnp.zeros((T, D), jnp.float32)
            for slot in range(SLOTS):
                p = jnp.exp2(s_ref[slot, rs, :] - m)
                for j in range(T // 128):
                    total = total + p[:, j * 128 : (j + 1) * 128]
                acc = acc + dot_nn(p.astype(jnp.bfloat16), kv[slot, 1])
            total = jnp.sum(total, axis=1, keepdims=True)
            out = (acc / total).astype(jnp.bfloat16)
            o_ref[rs, :] = out
            m_ref[rs, :] = jnp.broadcast_to(m + jnp.log2(total), (T, 128))
            delta = jnp.sum(
                g_ref[rs, :].astype(jnp.float32) * out.astype(jnp.float32), axis=1, keepdims=True
            )
            del_ref[rs, :] = jnp.broadcast_to(delta, (T, 128))
        return carry

    lax.fori_loop(0, heads // per, out_chunk, 0)

    def out_copy(src, dst, h, sem):
        return pltpu.make_async_copy(src.at[pl.ds(h * T, T), :], dst.at[:, pl.ds(h * D, D)], sem)

    for h in range(heads):
        out_copy(o_ref, o_hbm, h, out_sem.at[h]).start()

    def back_slot(i, carry):
        slot = jnp.where(i < 3, 6 + i, jnp.where(i < 6, i - 1, jnp.where(i == 6, 5, 8 - i)))
        kk = kv[slot, 0]
        vv = kv[slot, 1]
        dk = jnp.zeros((D, T), jnp.float32)
        dv = jnp.zeros((D, T), jnp.float32)
        step = 2 * T
        for b in range(R // step):
            rs = slice(b * step, (b + 1) * step)
            dp = dot_nt(g_ref[rs, :], vv)
            lse = m_ref[rs, :]
            delta = del_ref[rs, :]
            p = jnp.exp2(s_ref[slot, rs, :] - jnp.concatenate([lse, lse], axis=1))
            pb = p.astype(jnp.bfloat16)
            dsb = (p * (dp - jnp.concatenate([delta, delta], axis=1))).astype(jnp.bfloat16)
            dq_acc[rs, :] += dot_nn(dsb, kk)
            dv = dv + dot_nn(gt_ref[:, rs], pb)
            dk = dk + dot_nn(qt_ref[:, rs], dsb)
        part[0] = dk
        part[1] = dv

        @pl.when(i < 3)
        def _():
            gs[i] = part[...].astype(jnp.bfloat16)
            grad_to(i, partner).start()

        @pl.when((i >= 3) & (i < 6))
        def _():
            grad_to(i - 3, me).wait_recv()
            gs[i] = (part[...] + gr[i - 3].astype(jnp.float32)).astype(jnp.bfloat16)
            grad_to(i, row0 + 2 * lax.rem(y + 6 - i, ROWS_Y) + core).start()

        @pl.when(i == 6)
        def _():
            gs[6] = part[...].astype(jnp.bfloat16)
            grad_to(6, partner).start()

        @pl.when(i == 7)
        def _():
            total = part[...]
            for j in (3, 4, 5, 6):
                grad_to(j, me).wait_recv()
                mine = (y + (j - 2) >= ROWS_Y) if j < 6 else (core == 1)
                total = total + jnp.where(mine, gr[j].astype(jnp.float32), 0.0)
            gs[7] = total.astype(jnp.bfloat16)
            grad_to(7, z_prev).start()

        return carry

    lax.fori_loop(0, SLOTS, back_slot, 0)

    q_ref[...] = (dq_acc[...] * scale).astype(jnp.bfloat16)
    for h in range(heads):
        out_copy(q_ref, dq_hbm, h, out_sem.at[heads + h]).start()

    total = part[...]
    for j in (3, 4, 5, 6):
        mine = (y + (j - 2) < ROWS_Y) if j < 6 else (core == 0)
        total = total + jnp.where(mine, gr[j].astype(jnp.float32), 0.0)
    grad_to(7, me).wait_recv()
    total = total + gr[7].astype(jnp.float32)
    gk_ref[...] = (total[0] * scale).T.astype(jnp.bfloat16)
    gv_ref[...] = total[1].T.astype(jnp.bfloat16)

    for j in range(8):
        kv_to(0, 1 + j, me).wait_send()
        grad_to(j, me).wait_send()
    for h in range(heads):
        out_copy(o_ref, o_hbm, h, out_sem.at[h]).wait()
        out_copy(q_ref, dq_hbm, h, out_sem.at[heads + h]).wait()


def solution(mesh):
    n_seq = mesh.shape["seq"]

    def shards(queries, keys, values, lengths, grad_out):
        T, D = keys.shape
        heads = queries.shape[1] // D
        R = T * heads
        f32, bf16 = jnp.float32, jnp.bfloat16
        hbm = pl.BlockSpec(memory_space=pl.ANY)
        vmem = pl.BlockSpec(memory_space=pltpu.VMEM)
        smem = pl.BlockSpec(memory_space=pltpu.SMEM)
        dma = pltpu.SemaphoreType.DMA
        return pl.pallas_call(
            functools.partial(kernel, n_seq, heads),
            out_shape=(
                jax.ShapeDtypeStruct(queries.shape, bf16),
                jax.ShapeDtypeStruct(queries.shape, bf16),
                jax.ShapeDtypeStruct(keys.shape, bf16),
                jax.ShapeDtypeStruct(values.shape, bf16),
            ),
            in_specs=[smem, hbm, hbm, hbm, hbm],
            out_specs=(hbm, hbm, vmem, vmem),
            scratch_shapes=[
                pltpu.VMEM((R, D), bf16),
                pltpu.VMEM((R, D), bf16),
                pltpu.VMEM((D, R), bf16),
                pltpu.VMEM((D, R), bf16),
                pltpu.VMEM((SLOTS, 2, T, D), bf16),
                pltpu.VMEM((SLOTS, R, T), f32),
                pltpu.VMEM((R, 128), f32),
                pltpu.VMEM((R, 128), f32),
                pltpu.VMEM((R, D), f32),
                pltpu.VMEM((R, D), bf16),
                pltpu.VMEM((T, 128), jnp.int32),
                pltpu.VMEM((T, T), f32),
                pltpu.VMEM((2, D, T), f32),
                pltpu.VMEM((8, 2, D, T), bf16),
                pltpu.VMEM((8, 2, D, T), bf16),
                dma((2 + 2 * heads,)),
                dma((2 * heads,)),
                dma((SLOTS,)),
                dma((SLOTS,)),
                dma((8,)),
                dma((8,)),
            ],
            compiler_params=pltpu.CompilerParams(
                collective_id=0, has_side_effects=True, vmem_limit_bytes=67043328
            ),
        )(lengths, queries, keys, values, grad_out)

    spec = P(("dp", "seq"), None)
    return jax.shard_map(
        shards,
        mesh=mesh,
        in_specs=(spec, spec, spec, P("dp"), spec),
        out_specs=(spec, spec, spec, spec),
        check_vma=False,
    )
```

```python
import functools
import math

import jax
import jax.numpy as jnp
from jax import lax
from jax.experimental import pallas as pl
from jax.experimental.pallas import tpu as pltpu
from jax.sharding import PartitionSpec as P

NEG_FILL = -1e30
ROWS_Y = 4
SLOTS = 9


def dot_nt(a, b):
    return lax.dot_general(a, b, (((1,), (1,)), ((), ())), preferred_element_type=jnp.float32)


def dot_nn(a, b):
    return lax.dot_general(a, b, (((1,), (0,)), ((), ())), preferred_element_type=jnp.float32)


def kernel(
    n_seq,
    heads,
    len_ref,
    q_hbm,
    k_hbm,
    v_hbm,
    g_hbm,
    o_hbm,
    dq_hbm,
    gk_ref,
    gv_ref,
    q_ref,
    g_ref,
    qt_ref,
    gt_ref,
    kv,
    s_ref,
    m_ref,
    del_ref,
    dq_acc,
    o_ref,
    ds_ref,
    bias,
    part,
    gs,
    gr,
    in_sem,
    out_sem,
    kv_send,
    kv_recv,
    g_send,
    g_recv,
):
    T, D = gk_ref.shape
    R = T * heads
    half = D
    scale = 1.0 / math.sqrt(D)
    scale2 = scale * math.log2(math.e)
    me = lax.axis_index("seq")
    core = lax.rem(me, 2)
    y = lax.rem(me // 2, ROWS_Y)
    row0 = me - (y * 2 + core)
    partner = row0 + y * 2 + (1 - core)
    z_next = lax.rem(me + 2 * ROWS_Y, n_seq)
    z_prev = lax.rem(me + n_seq - 2 * ROWS_Y, n_seq)

    def y_dev(d):
        return row0 + 2 * lax.rem(y + d, ROWS_Y) + core

    def head_copy(src, dst, h, sem):
        return pltpu.make_async_copy(src.at[:, pl.ds(h * D, D)], dst.at[pl.ds(h * T, T), :], sem)

    k_copy = pltpu.make_async_copy(k_hbm, kv.at[0, 0], in_sem.at[0])
    v_copy = pltpu.make_async_copy(v_hbm, kv.at[0, 1], in_sem.at[1])
    k_copy.start()
    v_copy.start()
    for h in range(heads):
        head_copy(q_hbm, q_ref, h, in_sem.at[2 + h]).start()
    for h in range(heads):
        head_copy(g_hbm, g_ref, h, in_sem.at[2 + heads + h]).start()

    barrier = pltpu.get_barrier_semaphore()
    for dev in (z_next, z_prev, partner, y_dev(1), y_dev(2), y_dev(3)):
        pl.semaphore_signal(
            barrier, inc=1, device_id={"seq": dev}, device_id_type=pl.DeviceIdType.MESH
        )

    def kv_to(which, src, dst, dev):
        return pltpu.make_async_remote_copy(
            src_ref=kv.at[src, which],
            dst_ref=kv.at[dst, which],
            send_sem=kv_send.at[which, dst],
            recv_sem=kv_recv.at[which, dst],
            device_id={"seq": dev},
            device_id_type=pl.DeviceIdType.MESH,
        )

    def grad_to(i, dev):
        return pltpu.make_async_remote_copy(
            src_ref=gs.at[i],
            dst_ref=gr.at[i],
            send_sem=g_send.at[i],
            recv_sem=g_recv.at[i],
            device_id={"seq": dev},
            device_id_type=pl.DeviceIdType.MESH,
        )

    def own_to_row(which):
        for d in (1, 2, 3):

            @pl.when(y + d < ROWS_Y)
            def _():
                kv_to(which, 0, 2 + d, y_dev(d)).start()

        @pl.when(core == 0)
        def _():
            kv_to(which, 0, 2, partner).start()

    def back_to_row(which):
        for d in (1, 2, 3):

            @pl.when(y + d >= ROWS_Y)
            def _():
                kv_to(which, 1, 2 + d, y_dev(d)).start()

        @pl.when(core == 1)
        def _():
            kv_to(which, 1, 2, partner).start()

    def kv_wait(which, slot):
        kv_to(which, 0, slot, me).wait_recv()

    first = me * T
    pos = first + lax.broadcasted_iota(jnp.int32, (T, 128), 0)
    starts = jnp.zeros((T, 128), jnp.int32)
    end = jnp.int32(0)
    for i in range(len_ref.shape[0]):
        end = end + len_ref[i]
        starts = jnp.where(pos >= end, end, starts)
    ds_ref[...] = starts
    m_ref[...] = jnp.full(m_ref.shape, -3e38, jnp.float32)

    k_copy.wait()
    v_copy.wait()
    pl.semaphore_wait(barrier, 6)
    kv_to(0, 0, 1, z_next).start()
    own_to_row(0)
    kv_to(1, 0, 1, z_next).start()
    for h in range(heads):
        head_copy(q_hbm, q_ref, h, in_sem.at[2 + h]).wait()

    def score_slot(slot, carry):
        @pl.when(slot == 1)
        def _():
            dq_acc[...] = jnp.zeros(dq_acc.shape, jnp.float32)
            for h in range(heads):
                head_copy(g_hbm, g_ref, h, in_sem.at[2 + heads + h]).wait()
            w = R // 4
            for c in range(4):
                qt_ref[:, c * w : (c + 1) * w] = q_ref[c * w : (c + 1) * w, :].T
                gt_ref[:, c * w : (c + 1) * w] = g_ref[c * w : (c + 1) * w, :].T

        @pl.when(slot >= 1)
        def _():
            kv_wait(0, slot)

        @pl.when(slot == 1)
        def _():
            back_to_row(0)
            own_to_row(1)

        @pl.when((slot >= 3) & (slot <= 5))
        def _():
            kv_to(0, slot, slot + 3, partner).start()

        @pl.when(slot == 3)
        def _():
            kv_wait(1, 1)
            back_to_row(1)

        @pl.when(slot == 8)
        def _():
            for j in (3, 4, 5):
                kv_wait(1, j)
                kv_to(1, j, j + 3, partner).start()

        same = jnp.where(slot == 1, 2 * ROWS_Y, 2 * (slot - 2))
        same = jnp.where(slot == 0, 0, same)
        other = jnp.where(core == 1, 2 * (slot - 5) + 1, 2 * (slot - 5) - 1)
        near = jnp.where(core == 1, 1, 2 * ROWS_Y - 1)
        offset = jnp.where(slot >= 6, other, jnp.where(slot == 2, near, same))
        base = (me - offset) * T
        lo = ds_ref[...] - base
        hi = offset * T + lax.broadcasted_iota(jnp.int32, (T, 128), 0)
        col = lax.broadcasted_iota(jnp.int32, (T, 128), 1)
        for j in range(T // 128):
            cj = col + j * 128
            bias[:, j * 128 : (j + 1) * 128] = jnp.where(
                (cj >= lo) & (cj <= hi), 0.0, NEG_FILL
            )
        s = dot_nt(q_ref[...], kv[slot, 0]) * scale2
        for h in range(heads):
            rs = slice(h * T, (h + 1) * T)
            sh = s[rs] + bias[...]
            s_ref[slot, rs, :] = sh
            top = m_ref[rs, :]
            for j in range(T // 128):
                top = jnp.maximum(top, sh[:, j * 128 : (j + 1) * 128])
            m_ref[rs, :] = top
        return carry

    lax.fori_loop(0, SLOTS, score_slot, 0)

    for j in (2, 6, 7, 8):
        kv_wait(1, j)

    per = 4

    def out_chunk(c, carry):
        for u in range(per):
            rs = pl.ds(pl.multiple_of((c * per + u) * T, T), T)
            m = jnp.max(m_ref[rs, :], axis=1, keepdims=True)
            total = jnp.zeros((T, 128), jnp.float32)
            acc = jnp.zeros((T, D), jnp.float32)
            for slot in range(SLOTS):
                p = jnp.exp2(s_ref[slot, rs, :] - m)
                for j in range(T // 128):
                    total = total + p[:, j * 128 : (j + 1) * 128]
                acc = acc + dot_nn(p.astype(jnp.bfloat16), kv[slot, 1])
            total = jnp.sum(total, axis=1, keepdims=True)
            out = (acc / total).astype(jnp.bfloat16)
            o_ref[rs, :] = out
            m_ref[rs, :] = jnp.broadcast_to(m + jnp.log2(total), (T, 128))
            delta = jnp.sum(
                g_ref[rs, :].astype(jnp.float32) * out.astype(jnp.float32), axis=1, keepdims=True
            )
            del_ref[rs, :] = jnp.broadcast_to(delta, (T, 128))
        return carry

    lax.fori_loop(0, heads // per, out_chunk, 0)

    def out_copy(src, dst, h, sem):
        return pltpu.make_async_copy(src.at[pl.ds(h * T, T), :], dst.at[:, pl.ds(h * D, D)], sem)

    for h in range(heads):
        out_copy(o_ref, o_hbm, h, out_sem.at[h]).start()

    def back_slot(i, carry):
        slot = jnp.where(i < 3, 6 + i, jnp.where(i < 6, i, 8 - i))
        kk = kv[slot, 0]
        vv = kv[slot, 1]
        dk = jnp.zeros((D, T), jnp.float32)
        dv = jnp.zeros((D, T), jnp.float32)
        step = 2 * T
        for b in range(R // step):
            rs = slice(b * step, (b + 1) * step)
            dp = dot_nt(g_ref[rs, :], vv)
            lse = m_ref[rs, :]
            delta = del_ref[rs, :]
            p = jnp.exp2(s_ref[slot, rs, :] - jnp.concatenate([lse, lse], axis=1))
            pb = p.astype(jnp.bfloat16)
            dsb = (p * (dp - jnp.concatenate([delta, delta], axis=1))).astype(jnp.bfloat16)
            dq_acc[rs, :] += dot_nn(dsb, kk)
            dv = dv + dot_nn(gt_ref[:, rs], pb)
            dk = dk + dot_nn(qt_ref[:, rs], dsb)
        part[0] = dk
        part[1] = dv

        @pl.when(i < 3)
        def _():
            gs[i] = part[...].astype(jnp.bfloat16)
            grad_to(i, partner).start()

        @pl.when((i >= 3) & (i < 6))
        def _():
            grad_to(i - 3, me).wait_recv()
            gs[i] = (part[...] + gr[i - 3].astype(jnp.float32)).astype(jnp.bfloat16)
            grad_to(i, row0 + 2 * lax.rem(y + 6 - i, ROWS_Y) + core).start()

        @pl.when(i == 6)
        def _():
            gs[6] = part[...].astype(jnp.bfloat16)
            grad_to(6, partner).start()

        @pl.when(i == 7)
        def _():
            total = part[...]
            for j in (3, 4, 5, 6):
                grad_to(j, me).wait_recv()
                mine = (y + (j - 2) >= ROWS_Y) if j < 6 else (core == 1)
                total = total + jnp.where(mine, gr[j].astype(jnp.float32), 0.0)
            gs[7] = total.astype(jnp.bfloat16)
            grad_to(7, z_prev).start()

        return carry

    lax.fori_loop(0, SLOTS, back_slot, 0)

    q_ref[...] = (dq_acc[...] * scale).astype(jnp.bfloat16)
    for h in range(heads):
        out_copy(q_ref, dq_hbm, h, out_sem.at[heads + h]).start()

    total = part[...]
    for j in (3, 4, 5, 6):
        mine = (y + (j - 2) < ROWS_Y) if j < 6 else (core == 0)
        total = total + jnp.where(mine, gr[j].astype(jnp.float32), 0.0)
    grad_to(7, me).wait_recv()
    total = total + gr[7].astype(jnp.float32)
    gk_ref[...] = (total[0] * scale).T.astype(jnp.bfloat16)
    gv_ref[...] = total[1].T.astype(jnp.bfloat16)

    for j in range(8):
        kv_to(0, 0, 1 + j, me).wait_send()
        kv_to(1, 0, 1 + j, me).wait_send()
        grad_to(j, me).wait_send()
    for h in range(heads):
        out_copy(o_ref, o_hbm, h, out_sem.at[h]).wait()
        out_copy(q_ref, dq_hbm, h, out_sem.at[heads + h]).wait()


def solution(mesh):
    n_seq = mesh.shape["seq"]

    def shards(queries, keys, values, lengths, grad_out):
        T, D = keys.shape
        heads = queries.shape[1] // D
        R = T * heads
        f32, bf16 = jnp.float32, jnp.bfloat16
        hbm = pl.BlockSpec(memory_space=pl.ANY)
        vmem = pl.BlockSpec(memory_space=pltpu.VMEM)
        smem = pl.BlockSpec(memory_space=pltpu.SMEM)
        dma = pltpu.SemaphoreType.DMA
        return pl.pallas_call(
            functools.partial(kernel, n_seq, heads),
            out_shape=(
                jax.ShapeDtypeStruct(queries.shape, bf16),
                jax.ShapeDtypeStruct(queries.shape, bf16),
                jax.ShapeDtypeStruct(keys.shape, bf16),
                jax.ShapeDtypeStruct(values.shape, bf16),
            ),
            in_specs=[smem, hbm, hbm, hbm, hbm],
            out_specs=(hbm, hbm, vmem, vmem),
            scratch_shapes=[
                pltpu.VMEM((R, D), bf16),
                pltpu.VMEM((R, D), bf16),
                pltpu.VMEM((D, R), bf16),
                pltpu.VMEM((D, R), bf16),
                pltpu.VMEM((SLOTS, 2, T, D), bf16),
                pltpu.VMEM((SLOTS, R, T), f32),
                pltpu.VMEM((R, 128), f32),
                pltpu.VMEM((R, 128), f32),
                pltpu.VMEM((R, D), f32),
                pltpu.VMEM((R, D), bf16),
                pltpu.VMEM((T, 128), jnp.int32),
                pltpu.VMEM((T, T), f32),
                pltpu.VMEM((2, D, T), f32),
                pltpu.VMEM((8, 2, D, T), bf16),
                pltpu.VMEM((8, 2, D, T), bf16),
                dma((2 + 2 * heads,)),
                dma((2 * heads,)),
                dma((2, SLOTS)),
                dma((2, SLOTS)),
                dma((8,)),
                dma((8,)),
            ],
            compiler_params=pltpu.CompilerParams(
                collective_id=0, has_side_effects=True, vmem_limit_bytes=67043328
            ),
        )(lengths, queries, keys, values, grad_out)

    spec = P(("dp", "seq"), None)
    return jax.shard_map(
        shards,
        mesh=mesh,
        in_specs=(spec, spec, spec, P("dp"), spec),
        out_specs=(spec, spec, spec, spec),
        check_vma=False,
    )
```

```python
import functools
import math

import jax
import jax.numpy as jnp
from jax import lax
from jax.experimental import pallas as pl
from jax.experimental.pallas import tpu as pltpu
from jax.sharding import PartitionSpec as P

NEG_FILL = -1e30
ROWS_Y = 4
SLOTS = 9
PER1 = 16
PER2 = 8
PER3 = 8


def dot_nt(a, b):
    return lax.dot_general(a, b, (((1,), (1,)), ((), ())), preferred_element_type=jnp.float32)


def dot_nn(a, b):
    return lax.dot_general(a, b, (((1,), (0,)), ((), ())), preferred_element_type=jnp.float32)


def kernel(
    n_seq,
    heads,
    len_ref,
    q_hbm,
    k_hbm,
    v_hbm,
    g_hbm,
    o_out,
    dq_out,
    gk_ref,
    gv_ref,
    q_ref,
    g_ref,
    qt_ref,
    gt_ref,
    kv,
    s_ref,
    m_ref,
    del_ref,
    sum_ref,
    dq_acc,
    ds_ref,
    bias,
    p_ref,
    part,
    gs,
    gr,
    in_sem,
    kv_send,
    kv_recv,
    g_send,
    g_recv,
):
    T, D = gk_ref.shape
    R = T * heads
    half = D
    scale = 1.0 / math.sqrt(D)
    scale2 = scale * math.log2(math.e)
    me = lax.axis_index("seq")
    core = lax.rem(me, 2)
    y = lax.rem(me // 2, ROWS_Y)
    row0 = me - (y * 2 + core)
    partner = row0 + y * 2 + (1 - core)
    z_next = lax.rem(me + 2 * ROWS_Y, n_seq)
    z_prev = lax.rem(me + n_seq - 2 * ROWS_Y, n_seq)

    def y_dev(d):
        return row0 + 2 * lax.rem(y + d, ROWS_Y) + core

    def head_copy(src, dst, h, sem):
        return pltpu.make_async_copy(src.at[:, pl.ds(h * D, D)], dst.at[pl.ds(h * T, T), :], sem)

    k_copy = pltpu.make_async_copy(k_hbm, kv.at[0, 0], in_sem.at[0])
    v_copy = pltpu.make_async_copy(v_hbm, kv.at[0, 1], in_sem.at[1])
    k_copy.start()
    v_copy.start()
    for h in range(heads):
        head_copy(q_hbm, q_ref, h, in_sem.at[2 + h]).start()
    for h in range(heads):
        head_copy(g_hbm, g_ref, h, in_sem.at[2 + heads + h]).start()

    barrier = pltpu.get_barrier_semaphore()
    for dev in (z_next, z_prev, partner, y_dev(1), y_dev(2), y_dev(3)):
        pl.semaphore_signal(
            barrier, inc=1, device_id={"seq": dev}, device_id_type=pl.DeviceIdType.MESH
        )

    def kv_to(which, src, dst, dev):
        return pltpu.make_async_remote_copy(
            src_ref=kv.at[src, which],
            dst_ref=kv.at[dst, which],
            send_sem=kv_send.at[which, dst],
            recv_sem=kv_recv.at[which, dst],
            device_id={"seq": dev},
            device_id_type=pl.DeviceIdType.MESH,
        )

    def grad_to(i, dev):
        return pltpu.make_async_remote_copy(
            src_ref=gs.at[i],
            dst_ref=gr.at[i],
            send_sem=g_send.at[i],
            recv_sem=g_recv.at[i],
            device_id={"seq": dev},
            device_id_type=pl.DeviceIdType.MESH,
        )

    def own_to_row(which):
        for d in (1, 2, 3):

            @pl.when(y + d < ROWS_Y)
            def _():
                kv_to(which, 0, 2 + d, y_dev(d)).start()

        @pl.when(core == 0)
        def _():
            kv_to(which, 0, 2, partner).start()

    def back_to_row(which):
        for d in (1, 2, 3):

            @pl.when(y + d >= ROWS_Y)
            def _():
                kv_to(which, 1, 2 + d, y_dev(d)).start()

        @pl.when(core == 1)
        def _():
            kv_to(which, 1, 2, partner).start()

    def kv_wait(which, slot):
        kv_to(which, 0, slot, me).wait_recv()

    first = me * T
    pos = first + lax.broadcasted_iota(jnp.int32, (T, 128), 0)
    starts = jnp.zeros((T, 128), jnp.int32)
    end = jnp.int32(0)
    for i in range(len_ref.shape[0]):
        end = end + len_ref[i]
        starts = jnp.where(pos >= end, end, starts)
    ds_ref[...] = starts
    m_ref[...] = jnp.full(m_ref.shape, -3e38, jnp.float32)

    def score_slot(slot):
        same = jnp.where(slot == 1, 2 * ROWS_Y, 2 * (slot - 2))
        same = jnp.where(slot == 0, 0, same)
        other = jnp.where(core == 1, 2 * (slot - 5) + 1, 2 * (slot - 5) - 1)
        near = jnp.where(core == 1, 1, 2 * ROWS_Y - 1)
        offset = jnp.where(slot >= 6, other, jnp.where(slot == 2, near, same))
        base = (me - offset) * T
        lo = ds_ref[...] - base
        hi = offset * T + lax.broadcasted_iota(jnp.int32, (T, 128), 0)
        col = lax.broadcasted_iota(jnp.int32, (T, 128), 1)
        for j in range(T // 128):
            cj = col + j * 128
            bias[:, j * 128 : (j + 1) * 128] = jnp.where(
                (cj >= lo) & (cj <= hi), 0.0, NEG_FILL
            )
        s = dot_nt(q_ref[...], kv[slot, 0]) * scale2
        for h in range(heads):
            rs = slice(h * T, (h + 1) * T)
            sh = s[rs] + bias[...]
            s_ref[slot, rs, :] = sh
            top = m_ref[rs, :]
            for j in range(T // 128):
                top = jnp.maximum(top, sh[:, j * 128 : (j + 1) * 128])
            m_ref[rs, :] = top

    def out_group(slots, place, per):
        def weights(h, rs):
            m = jnp.max(m_ref[rs, :], axis=1, keepdims=True)
            total = jnp.zeros((T, 128), jnp.float32)
            for n, slot in enumerate(slots):
                p = jnp.exp2(s_ref[slot, rs, :] - m)
                for j in range(T // 128):
                    total = total + p[:, j * 128 : (j + 1) * 128]
                p_ref[h % 2, :, n * T : (n + 1) * T] = p.astype(jnp.bfloat16)
            if place > 0:
                alpha = jnp.exp2(del_ref[rs, :] - m)
                total = total + sum_ref[rs, :] * alpha
                dq_acc[rs, :] = dq_acc[rs, :] * alpha
            sum_ref[rs, :] = total
            if place < 2:
                del_ref[rs, :] = jnp.broadcast_to(m, (T, 128))
            else:
                m_ref[rs, :] = jnp.broadcast_to(m, (T, 128))

        def outputs(h, rs, col):
            acc = jnp.zeros((T, D), jnp.float32)
            for n, slot in enumerate(slots):
                acc = acc + dot_nn(p_ref[h % 2, :, n * T : (n + 1) * T], kv[slot, 1])
            if place > 0:
                acc = acc + dq_acc[rs, :]
            if place < 2:
                dq_acc[rs, :] = acc
                return
            total = jnp.sum(sum_ref[rs, :], axis=1, keepdims=True)
            dq_acc[rs, :] = jnp.zeros((T, D), jnp.float32)
            out = (acc / total).astype(jnp.bfloat16)
            o_out[:, pl.ds(pl.multiple_of(col, D), D)] = out
            m_ref[rs, :] = m_ref[rs, :] + jnp.log2(total)
            delta = jnp.sum(
                g_ref[rs, :].astype(jnp.float32) * out.astype(jnp.float32), axis=1, keepdims=True
            )
            del_ref[rs, :] = jnp.broadcast_to(delta, (T, 128))

        def heads_of(c, carry):
            rows = [pl.ds(pl.multiple_of((c * per + h) * T, T), T) for h in range(per)]
            weights(0, rows[0])
            for h in range(per):
                if h + 1 < per:
                    weights(h + 1, rows[h + 1])
                outputs(h, rows[h], (c * per + h) * D)
            return carry

        if per == heads:
            heads_of(0, 0)
        else:
            lax.fori_loop(0, heads // per, heads_of, 0)

    for h in range(heads):
        head_copy(q_hbm, q_ref, h, in_sem.at[2 + h]).wait()
    k_copy.wait()
    v_copy.wait()
    score_slot(0)
    pl.semaphore_wait(barrier, 6)
    kv_to(0, 0, 1, z_next).start()
    own_to_row(0)
    kv_to(1, 0, 1, z_next).start()
    own_to_row(1)
    for h in range(heads):
        head_copy(g_hbm, g_ref, h, in_sem.at[2 + heads + h]).wait()
    w = R // 4
    for c in range(4):
        qt_ref[:, c * w : (c + 1) * w] = q_ref[c * w : (c + 1) * w, :].T
        gt_ref[:, c * w : (c + 1) * w] = g_ref[c * w : (c + 1) * w, :].T

    def near_slot(slot, carry):
        kv_wait(0, slot)

        @pl.when(slot == 1)
        def _():
            back_to_row(0)

        @pl.when(slot == 2)
        def _():
            kv_wait(1, 1)
            back_to_row(1)

        score_slot(slot)
        return carry

    lax.fori_loop(1, 3, near_slot, 0)
    out_group((0, 1), 0, PER1)

    def far_slot(slot, carry):
        kv_wait(0, slot)

        @pl.when(slot <= 5)
        def _():
            kv_to(0, slot, slot + 3, partner).start()

        @pl.when(slot == 7)
        def _():
            for j in (3, 4, 5):
                kv_wait(1, j)
                kv_to(1, j, j + 3, partner).start()

        score_slot(slot)
        return carry

    lax.fori_loop(3, SLOTS, far_slot, 0)
    kv_wait(1, 2)
    out_group((2, 3, 4, 5), 1, PER2)
    for j in (6, 7, 8):
        kv_wait(1, j)
    out_group((6, 7, 8), 2, PER3)

    def back_slot(i, carry):
        slot = jnp.where(i < 3, 6 + i, jnp.where(i < 6, i, 8 - i))
        kk = kv[slot, 0]
        vv = kv[slot, 1]
        dk = jnp.zeros((D, T), jnp.float32)
        dv = jnp.zeros((D, T), jnp.float32)
        step = 2 * T
        for b in range(R // step):
            rs = slice(b * step, (b + 1) * step)
            dp = dot_nt(g_ref[rs, :], vv)
            lse = m_ref[rs, :]
            delta = del_ref[rs, :]
            p = jnp.exp2(s_ref[slot, rs, :] - jnp.concatenate([lse, lse], axis=1))
            pb = p.astype(jnp.bfloat16)
            dsb = (p * (dp - jnp.concatenate([delta, delta], axis=1))).astype(jnp.bfloat16)
            dq_acc[rs, :] += dot_nn(dsb, kk)
            dv = dv + dot_nn(gt_ref[:, rs], pb)
            dk = dk + dot_nn(qt_ref[:, rs], dsb)
        part[0] = dk
        part[1] = dv

        @pl.when(i < 3)
        def _():
            gs[i] = part[...].astype(jnp.bfloat16)
            grad_to(i, partner).start()

        @pl.when((i >= 3) & (i < 6))
        def _():
            grad_to(i - 3, me).wait_recv()
            gs[i] = (part[...] + gr[i - 3].astype(jnp.float32)).astype(jnp.bfloat16)
            grad_to(i, row0 + 2 * lax.rem(y + 6 - i, ROWS_Y) + core).start()

        @pl.when(i == 6)
        def _():
            gs[6] = part[...].astype(jnp.bfloat16)
            grad_to(6, partner).start()

        @pl.when(i == 7)
        def _():
            total = part[...]
            for j in (3, 4, 5, 6):
                grad_to(j, me).wait_recv()
                mine = (y + (j - 2) >= ROWS_Y) if j < 6 else (core == 1)
                total = total + jnp.where(mine, gr[j].astype(jnp.float32), 0.0)
            gs[7] = total.astype(jnp.bfloat16)
            grad_to(7, z_prev).start()

        return carry

    lax.fori_loop(0, SLOTS, back_slot, 0)

    for h in range(heads):
        dq_out[:, h * D : (h + 1) * D] = (dq_acc[h * T : (h + 1) * T, :] * scale).astype(jnp.bfloat16)

    total = part[...]
    for j in (3, 4, 5, 6):
        mine = (y + (j - 2) < ROWS_Y) if j < 6 else (core == 0)
        total = total + jnp.where(mine, gr[j].astype(jnp.float32), 0.0)
    grad_to(7, me).wait_recv()
    total = total + gr[7].astype(jnp.float32)
    gk_ref[...] = (total[0] * scale).T.astype(jnp.bfloat16)
    gv_ref[...] = total[1].T.astype(jnp.bfloat16)

    for j in range(8):
        kv_to(0, 0, 1 + j, me).wait_send()
        kv_to(1, 0, 1 + j, me).wait_send()
        grad_to(j, me).wait_send()


def solution(mesh):
    n_seq = mesh.shape["seq"]

    def shards(queries, keys, values, lengths, grad_out):
        T, D = keys.shape
        heads = queries.shape[1] // D
        R = T * heads
        f32, bf16 = jnp.float32, jnp.bfloat16
        hbm = pl.BlockSpec(memory_space=pl.ANY)
        vmem = pl.BlockSpec(memory_space=pltpu.VMEM)
        smem = pl.BlockSpec(memory_space=pltpu.SMEM)
        dma = pltpu.SemaphoreType.DMA
        results = pl.pallas_call(
            functools.partial(kernel, n_seq, heads),
            out_shape=tuple(
                pltpu.VMEM(x.shape, bf16) for x in (queries, queries, keys, values)
            ),
            in_specs=[smem, hbm, hbm, hbm, hbm],
            out_specs=(vmem,) * 4,
            scratch_shapes=[
                pltpu.VMEM((R, D), bf16),
                pltpu.VMEM((R, D), bf16),
                pltpu.VMEM((D, R), bf16),
                pltpu.VMEM((D, R), bf16),
                pltpu.VMEM((SLOTS, 2, T, D), bf16),
                pltpu.VMEM((SLOTS, R, T), f32),
                pltpu.VMEM((R, 128), f32),
                pltpu.VMEM((R, 128), f32),
                pltpu.VMEM((R, 128), f32),
                pltpu.VMEM((R, D), f32),
                pltpu.VMEM((T, 128), jnp.int32),
                pltpu.VMEM((T, T), f32),
                pltpu.VMEM((2, T, 4 * T), bf16),
                pltpu.VMEM((2, D, T), f32),
                pltpu.VMEM((8, 2, D, T), bf16),
                pltpu.VMEM((8, 2, D, T), bf16),
                dma((2 + 2 * heads,)),
                dma((2, SLOTS)),
                dma((2, SLOTS)),
                dma((8,)),
                dma((8,)),
            ],
            compiler_params=pltpu.CompilerParams(
                collective_id=0, has_side_effects=True, vmem_limit_bytes=64487424
            ),
        )(lengths, queries, keys, values, grad_out)
        return results

    spec = P(("dp", "seq"), None)
    return jax.shard_map(
        shards,
        mesh=mesh,
        in_specs=(spec, spec, spec, P("dp"), spec),
        out_specs=(spec, spec, spec, spec),
        check_vma=False,
    )
```

```python
import functools
import math

import jax
import jax.numpy as jnp
from jax import lax
from jax.experimental import pallas as pl
from jax.experimental.pallas import tpu as pltpu
from jax.sharding import PartitionSpec as P

NEG_FILL = -1e30
ROWS_Y = 4
SLOTS = 9
PER1 = 16
PER2 = 8
PER3 = 8


def dot_nt(a, b):
    return lax.dot_general(a, b, (((1,), (1,)), ((), ())), preferred_element_type=jnp.float32)


def dot_nn(a, b):
    return lax.dot_general(a, b, (((1,), (0,)), ((), ())), preferred_element_type=jnp.float32)


def kernel(
    n_seq,
    heads,
    len_ref,
    q_hbm,
    k_hbm,
    v_hbm,
    g_hbm,
    o_out,
    dq_out,
    gk_ref,
    gv_ref,
    q_ref,
    g_ref,
    qt_ref,
    gt_ref,
    kv,
    s_ref,
    m_ref,
    del_ref,
    sum_ref,
    dq_acc,
    ds_ref,
    bias,
    p_ref,
    part,
    gs,
    gr,
    in_sem,
    kv_send,
    kv_recv,
    g_send,
    g_recv,
):
    T, D = gk_ref.shape
    R = T * heads
    half = D
    scale = 1.0 / math.sqrt(D)
    scale2 = scale * math.log2(math.e)
    me = lax.axis_index("seq")
    core = lax.rem(me, 2)
    y = lax.rem(me // 2, ROWS_Y)
    row0 = me - (y * 2 + core)
    partner = row0 + y * 2 + (1 - core)
    z_next = lax.rem(me + 2 * ROWS_Y, n_seq)
    z_prev = lax.rem(me + n_seq - 2 * ROWS_Y, n_seq)

    def y_dev(d):
        return row0 + 2 * lax.rem(y + d, ROWS_Y) + core

    def head_copy(src, dst, h, sem):
        return pltpu.make_async_copy(src.at[:, pl.ds(h * D, D)], dst.at[pl.ds(h * T, T), :], sem)

    k_copy = pltpu.make_async_copy(k_hbm, kv.at[0, 0], in_sem.at[0])
    v_copy = pltpu.make_async_copy(v_hbm, kv.at[0, 1], in_sem.at[1])
    k_copy.start()
    v_copy.start()
    for h in range(heads):
        head_copy(q_hbm, q_ref, h, in_sem.at[2 + h]).start()
    for h in range(heads):
        head_copy(g_hbm, g_ref, h, in_sem.at[2 + heads + h]).start()

    barrier = pltpu.get_barrier_semaphore()
    for dev in (z_next, z_prev, partner, y_dev(1), y_dev(2), y_dev(3)):
        pl.semaphore_signal(
            barrier, inc=1, device_id={"seq": dev}, device_id_type=pl.DeviceIdType.MESH
        )

    def kv_to(which, src, dst, dev):
        return pltpu.make_async_remote_copy(
            src_ref=kv.at[src, which],
            dst_ref=kv.at[dst, which],
            send_sem=kv_send.at[which, dst],
            recv_sem=kv_recv.at[which, dst],
            device_id={"seq": dev},
            device_id_type=pl.DeviceIdType.MESH,
        )

    def grad_to(i, dev):
        return pltpu.make_async_remote_copy(
            src_ref=gs.at[i],
            dst_ref=gr.at[i],
            send_sem=g_send.at[i],
            recv_sem=g_recv.at[i],
            device_id={"seq": dev},
            device_id_type=pl.DeviceIdType.MESH,
        )

    def own_to_row(which):
        for d in (1, 2, 3):

            @pl.when(y + d < ROWS_Y)
            def _():
                kv_to(which, 0, 2 + d, y_dev(d)).start()

        @pl.when(core == 0)
        def _():
            kv_to(which, 0, 2, partner).start()

    def back_to_row(which):
        for d in (1, 2, 3):

            @pl.when(y + d >= ROWS_Y)
            def _():
                kv_to(which, 1, 2 + d, y_dev(d)).start()

        @pl.when(core == 1)
        def _():
            kv_to(which, 1, 2, partner).start()

    def kv_wait(which, slot):
        kv_to(which, 0, slot, me).wait_recv()

    first = me * T
    pos = first + lax.broadcasted_iota(jnp.int32, (T, 128), 0)
    starts = jnp.zeros((T, 128), jnp.int32)
    end = jnp.int32(0)
    for i in range(len_ref.shape[0]):
        end = end + len_ref[i]
        starts = jnp.where(pos >= end, end, starts)
    ds_ref[...] = starts
    m_ref[...] = jnp.full(m_ref.shape, -3e38, jnp.float32)

    def score_slot(slot):
        same = jnp.where(slot == 1, 2 * ROWS_Y, 2 * (slot - 2))
        same = jnp.where(slot == 0, 0, same)
        other = jnp.where(core == 1, 2 * (slot - 5) + 1, 2 * (slot - 5) - 1)
        near = jnp.where(core == 1, 1, 2 * ROWS_Y - 1)
        offset = jnp.where(slot >= 6, other, jnp.where(slot == 2, near, same))
        base = (me - offset) * T
        lo = ds_ref[...] - base
        hi = offset * T + lax.broadcasted_iota(jnp.int32, (T, 128), 0)
        col = lax.broadcasted_iota(jnp.int32, (T, 128), 1)
        for j in range(T // 128):
            cj = col + j * 128
            bias[:, j * 128 : (j + 1) * 128] = jnp.where(
                (cj >= lo) & (cj <= hi), 0.0, NEG_FILL
            )
        s = dot_nt(q_ref[...], kv[slot, 0]) * scale2
        for h in range(heads):
            rs = slice(h * T, (h + 1) * T)
            sh = s[rs] + bias[...]
            s_ref[slot, rs, :] = sh
            top = m_ref[rs, :]
            for j in range(T // 128):
                top = jnp.maximum(top, sh[:, j * 128 : (j + 1) * 128])
            m_ref[rs, :] = top

    def out_group(slots, place, per):
        def weights(h, rs):
            m = jnp.max(m_ref[rs, :], axis=1, keepdims=True)
            total = jnp.zeros((T, 128), jnp.float32)
            for n, slot in enumerate(slots):
                p = jnp.exp2(s_ref[slot, rs, :] - m)
                for j in range(T // 128):
                    total = total + p[:, j * 128 : (j + 1) * 128]
                p_ref[h % 2, :, n * T : (n + 1) * T] = p.astype(jnp.bfloat16)
            if place > 0:
                alpha = jnp.exp2(del_ref[rs, :] - m)
                total = total + sum_ref[rs, :] * alpha
                dq_acc[rs, :] = dq_acc[rs, :] * alpha
            sum_ref[rs, :] = total
            if place < 2:
                del_ref[rs, :] = jnp.broadcast_to(m, (T, 128))
            else:
                m_ref[rs, :] = jnp.broadcast_to(m, (T, 128))

        def outputs(h, rs, col):
            acc = jnp.zeros((T, D), jnp.float32)
            for n, slot in enumerate(slots):
                acc = acc + dot_nn(p_ref[h % 2, :, n * T : (n + 1) * T], kv[slot, 1])
            if place > 0:
                acc = acc + dq_acc[rs, :]
            if place < 2:
                dq_acc[rs, :] = acc
                return
            total = jnp.sum(sum_ref[rs, :], axis=1, keepdims=True)
            dq_acc[rs, :] = jnp.zeros((T, D), jnp.float32)
            out = (acc / total).astype(jnp.bfloat16)
            o_out[:, pl.ds(pl.multiple_of(col, D), D)] = out
            m_ref[rs, :] = m_ref[rs, :] + jnp.log2(total)
            delta = jnp.sum(
                g_ref[rs, :].astype(jnp.float32) * out.astype(jnp.float32), axis=1, keepdims=True
            )
            del_ref[rs, :] = jnp.broadcast_to(delta, (T, 128))

        def heads_of(c, carry):
            rows = [pl.ds(pl.multiple_of((c * per + h) * T, T), T) for h in range(per)]
            weights(0, rows[0])
            for h in range(per):
                if h + 1 < per:
                    weights(h + 1, rows[h + 1])
                outputs(h, rows[h], (c * per + h) * D)
            return carry

        if per == heads:
            heads_of(0, 0)
        else:
            lax.fori_loop(0, heads // per, heads_of, 0)

    for h in range(heads):
        head_copy(q_hbm, q_ref, h, in_sem.at[2 + h]).wait()
    k_copy.wait()
    v_copy.wait()
    for h in range(heads):
        head_copy(g_hbm, g_ref, h, in_sem.at[2 + heads + h]).wait()
    w = R // 4
    for c in range(4):
        qt_ref[:, c * w : (c + 1) * w] = q_ref[c * w : (c + 1) * w, :].T
        gt_ref[:, c * w : (c + 1) * w] = g_ref[c * w : (c + 1) * w, :].T
    pl.semaphore_wait(barrier, 6)
    kv_to(0, 0, 1, z_next).start()
    own_to_row(0)
    kv_to(1, 0, 1, z_next).start()
    score_slot(0)
    own_to_row(1)

    def near_slot(slot, carry):
        kv_wait(0, slot)

        @pl.when(slot == 1)
        def _():
            back_to_row(0)

        @pl.when(slot == 2)
        def _():
            kv_wait(1, 1)
            back_to_row(1)

        score_slot(slot)
        return carry

    lax.fori_loop(1, 3, near_slot, 0)
    out_group((0, 1), 0, PER1)

    def far_slot(slot, carry):
        kv_wait(0, slot)

        @pl.when(slot <= 5)
        def _():
            kv_to(0, slot, slot + 3, partner).start()

        @pl.when(slot == 7)
        def _():
            for j in (3, 4, 5):
                kv_wait(1, j)
                kv_to(1, j, j + 3, partner).start()

        score_slot(slot)
        return carry

    lax.fori_loop(3, SLOTS, far_slot, 0)
    kv_wait(1, 2)
    out_group((2, 3, 4, 5), 1, PER2)
    for j in (6, 7, 8):
        kv_wait(1, j)
    out_group((6, 7, 8), 2, PER3)

    def back_slot(i, carry):
        slot = jnp.where(i < 3, 6 + i, jnp.where(i < 6, i, 8 - i))
        kk = kv[slot, 0]
        vv = kv[slot, 1]
        dk = jnp.zeros((D, T), jnp.float32)
        dv = jnp.zeros((D, T), jnp.float32)
        step = 2 * T
        for b in range(R // step):
            rs = slice(b * step, (b + 1) * step)
            dp = dot_nt(g_ref[rs, :], vv)
            lse = m_ref[rs, :]
            delta = del_ref[rs, :]
            p = jnp.exp2(s_ref[slot, rs, :] - jnp.concatenate([lse, lse], axis=1))
            pb = p.astype(jnp.bfloat16)
            dsb = (p * (dp - jnp.concatenate([delta, delta], axis=1))).astype(jnp.bfloat16)
            dq_acc[rs, :] += dot_nn(dsb, kk)
            dv = dv + dot_nn(gt_ref[:, rs], pb)
            dk = dk + dot_nn(qt_ref[:, rs], dsb)
        part[0] = dk
        part[1] = dv

        @pl.when(i < 3)
        def _():
            gs[i] = part[...].astype(jnp.bfloat16)
            grad_to(i, partner).start()

        @pl.when((i >= 3) & (i < 6))
        def _():
            grad_to(i - 3, me).wait_recv()
            gs[i] = (part[...] + gr[i - 3].astype(jnp.float32)).astype(jnp.bfloat16)
            grad_to(i, row0 + 2 * lax.rem(y + 6 - i, ROWS_Y) + core).start()

        @pl.when(i == 6)
        def _():
            gs[6] = part[...].astype(jnp.bfloat16)
            grad_to(6, partner).start()

        @pl.when(i == 7)
        def _():
            total = part[...]
            for j in (3, 4, 5, 6):
                grad_to(j, me).wait_recv()
                mine = (y + (j - 2) >= ROWS_Y) if j < 6 else (core == 1)
                total = total + jnp.where(mine, gr[j].astype(jnp.float32), 0.0)
            gs[7] = total.astype(jnp.bfloat16)
            grad_to(7, z_prev).start()

        return carry

    lax.fori_loop(0, SLOTS, back_slot, 0)

    for h in range(heads):
        dq_out[:, h * D : (h + 1) * D] = (dq_acc[h * T : (h + 1) * T, :] * scale).astype(jnp.bfloat16)

    total = part[...]
    for j in (3, 4, 5, 6):
        mine = (y + (j - 2) < ROWS_Y) if j < 6 else (core == 0)
        total = total + jnp.where(mine, gr[j].astype(jnp.float32), 0.0)
    grad_to(7, me).wait_recv()
    total = total + gr[7].astype(jnp.float32)
    gk_ref[...] = (total[0] * scale).T.astype(jnp.bfloat16)
    gv_ref[...] = total[1].T.astype(jnp.bfloat16)

    for j in range(8):
        kv_to(0, 0, 1 + j, me).wait_send()
        kv_to(1, 0, 1 + j, me).wait_send()
        grad_to(j, me).wait_send()


def solution(mesh):
    n_seq = mesh.shape["seq"]

    def shards(queries, keys, values, lengths, grad_out):
        T, D = keys.shape
        heads = queries.shape[1] // D
        R = T * heads
        f32, bf16 = jnp.float32, jnp.bfloat16
        hbm = pl.BlockSpec(memory_space=pl.ANY)
        vmem = pl.BlockSpec(memory_space=pltpu.VMEM)
        smem = pl.BlockSpec(memory_space=pltpu.SMEM)
        dma = pltpu.SemaphoreType.DMA
        results = pl.pallas_call(
            functools.partial(kernel, n_seq, heads),
            out_shape=tuple(
                pltpu.VMEM(x.shape, bf16) for x in (queries, queries, keys, values)
            ),
            in_specs=[smem, hbm, hbm, hbm, hbm],
            out_specs=(vmem,) * 4,
            scratch_shapes=[
                pltpu.VMEM((R, D), bf16),
                pltpu.VMEM((R, D), bf16),
                pltpu.VMEM((D, R), bf16),
                pltpu.VMEM((D, R), bf16),
                pltpu.VMEM((SLOTS, 2, T, D), bf16),
                pltpu.VMEM((SLOTS, R, T), f32),
                pltpu.VMEM((R, 128), f32),
                pltpu.VMEM((R, 128), f32),
                pltpu.VMEM((R, 128), f32),
                pltpu.VMEM((R, D), f32),
                pltpu.VMEM((T, 128), jnp.int32),
                pltpu.VMEM((T, T), f32),
                pltpu.VMEM((2, T, 4 * T), bf16),
                pltpu.VMEM((2, D, T), f32),
                pltpu.VMEM((8, 2, D, T), bf16),
                pltpu.VMEM((8, 2, D, T), bf16),
                dma((2 + 2 * heads,)),
                dma((2, SLOTS)),
                dma((2, SLOTS)),
                dma((8,)),
                dma((8,)),
            ],
            compiler_params=pltpu.CompilerParams(
                collective_id=0, has_side_effects=True, vmem_limit_bytes=64487424
            ),
        )(lengths, queries, keys, values, grad_out)
        return results

    spec = P(("dp", "seq"), None)
    return jax.shard_map(
        shards,
        mesh=mesh,
        in_specs=(spec, spec, spec, P("dp"), spec),
        out_specs=(spec, spec, spec, spec),
        check_vma=False,
    )
```
